32 devices in a mesh: row: 4 (over y, core), col: 8 (over z, x).
Axes of the slice: x: 2, y: 2, z: 4, core: 2. Of those that a mesh axis runs over, the one named last changes fastest.
Arguments:
- left_derivatives: bfloat16 [256, 512, 512], P(('row', 'col')), may hold values from -0.25 to 0.25
- right_derivatives: bfloat16 [256, 512, 512], P(('row', 'col')), may hold values from -0.25 to 0.25
- bundle_tile_slot: int32 [256], P(('row', 'col')), may hold values from 0 to 511, as said below
- tile_pos: int32 [4, 8, 16], P('row', 'col'), may hold values from 0 to 511, as said below
- right_sides: float32 [16, 65536], P(None, ('row', 'col')), may hold values from -6 to 6
- diagonal: float32 [65536], P(('row', 'col')), may hold values from 0.8 to 3
Outputs:
- solution: float32 [16, 65536], P(None, ('row', 'col'))
The draws below stay inside these ranges and needn't reach their ends.
Inputs may be any that keep to these rules, and one draw needn't show every extreme that they name: `bundle_tile_slot`: bundle b lies on the device of index b // 8 along row+col. The slot g that it names belongs to a device of the same row index. Of the bundles of one device, at most 2 name slots of any one device, and in each row some device is named exactly 2 times by the bundles of every device of that row. `tile_pos`: the 16 entries of one device are distinct.
All inputs are finite; a program needn't handle non-finite values.
Results may differ from the reference program's by a relative error of at most 0.002.
Values may be sent and summed in bfloat16 or wider, within the bound.
A program may use at most 192 MiB of HBM per device.

```python
import math
import jax
import jax.numpy as jnp
from jax import lax

BLOCK_PARAMS = 512
MEASURE_ROWS = 512
NRHS = 16
BLK_DEV = 4
CAP = 16
SEND_CAP = 2
ITERS = 3
BUN_DEV = 8
BLOCKS = 128
ORDER = 65536
BUNDLE_TOTAL = 256
N_ROW = 4
N_COL = 8


def slot_counts(key):
    lowest = CAP - CAP // 2
    return jax.random.randint(jax.random.fold_in(key, 101), (N_ROW * N_COL,), lowest, CAP + 1)


def draw_tile_pos(key, part):
    devices = N_ROW * N_COL
    positions = devices * BLK_DEV * BLK_DEV
    device_keys = jax.random.split(jax.random.fold_in(key, 7), devices)

    def choose(device_key):
        return jax.random.permutation(device_key, positions)[:CAP]
    picked = jax.vmap(choose)(device_keys)
    return picked.reshape(N_ROW, N_COL, CAP).astype(jnp.int32)


def draw_bundle_tile_slot(key, part):
    devices = N_ROW * N_COL
    counts = slot_counts(key)
    hottest = jax.random.randint(jax.random.fold_in(key, 103), (N_ROW,), 0, N_COL)
    device_keys = jax.random.split(jax.random.fold_in(key, 107), devices)
    candidates = SEND_CAP * N_COL
    column_of = jnp.arange(candidates, dtype=jnp.int32) // SEND_CAP

    def one_device(device, device_key):
        band_row = device // N_COL
        key_order, key_shuffle, key_slot = jax.random.split(device_key, 3)
        ranking = jax.random.permutation(key_order, candidates).astype(jnp.int32)
        ranking = jnp.where(column_of == hottest[band_row], ranking - candidates, ranking)
        bundle_ordering = jnp.argsort(ranking, stable=True)
        targets = column_of[bundle_ordering[:BUN_DEV]]
        targets = targets[jax.random.permutation(key_shuffle, BUN_DEV)]
        owners = band_row * N_COL + targets
        within = jax.random.randint(key_slot, (BUN_DEV,), 0, counts[owners])
        return owners * CAP + within
    bundle_ids = jax.vmap(one_device)(jnp.arange(devices, dtype=jnp.int32), device_keys)
    return bundle_ids.reshape(-1).astype(jnp.int32)


def steps_of(stream_key, extent, pieces, low, largest):
    factor_of, own = 1.0, jax.random.fold_in(stream_key, 6)
    for axis_at, shards_of in pieces:
        heights = jnp.exp(jax.random.uniform(jax.random.fold_in(own, axis_at), (shards_of,), jnp.float32, low / len(pieces), largest / len(pieces)))
        factor_of = factor_of * jnp.repeat(heights, extent[axis_at] // shards_of).reshape([-1 if axis == axis_at else 1 for axis in range(len(extent))])
    return factor_of


def normal_values(stream_key, shape, deviation, reach, pieces=(), kind=jnp.bfloat16):
    values = jax.random.normal(stream_key, shape, jnp.float32) * deviation
    if len(pieces) > 0:
        values = steps_of(stream_key, shape, pieces, -0.22, 0.18) * values
    return jnp.clip(values, min=-reach, max=reach).astype(kind)


def setup_inputs(seed: int = 0) -> dict:
    keys = jax.random.split(jax.random.key(seed), 7)
    return {
        "left_derivatives": normal_values(keys[0], (BUNDLE_TOTAL, MEASURE_ROWS, BLOCK_PARAMS), (0.4 / (BLOCK_PARAMS * MEASURE_ROWS) ** 0.25), 0.25, ((0, 32),)),
        "right_derivatives": normal_values(keys[1], (BUNDLE_TOTAL, MEASURE_ROWS, BLOCK_PARAMS), (0.4 / (BLOCK_PARAMS * MEASURE_ROWS) ** 0.25), 0.25, ((0, 32),)),
        "bundle_tile_slot": draw_bundle_tile_slot(jax.random.fold_in(keys[6], 71), 0),
        "tile_pos": draw_tile_pos(jax.random.fold_in(keys[6], 71), 0),
        "right_sides": normal_values(keys[4], (NRHS, ORDER), 1.0, 6.0, ((1, 32),), jnp.float32),
        "diagonal": jnp.clip(jnp.exp(math.log(3.0) - 1.3217558 * jax.random.uniform(keys[5], (ORDER,), jnp.float32) ** steps_of(keys[5], (ORDER,), ((0, 32),), -0.2, 0.2)), 0.8, 3.0),
    }


highest = lax.Precision.HIGHEST

def build_matrix(left_derivatives, right_derivatives, bundle_tile_slot):
    slot_total = N_ROW * N_COL * CAP

    def add_bundle(matrix, bundle):
        left_panel, right_panel, target = bundle
        product = jnp.dot(left_panel.T, right_panel, preferred_element_type=jnp.float32).astype(jnp.bfloat16)
        product = lax.optimization_barrier(product).astype(jnp.float32)
        return (matrix.at[target].add(product), None)
    empty = jnp.zeros((slot_total, BLOCK_PARAMS, BLOCK_PARAMS), jnp.float32)
    matrix, ignored = lax.scan(add_bundle, empty, (left_derivatives, right_derivatives, bundle_tile_slot.astype(jnp.int32)))
    return matrix

def block_places(tile_pos):
    slot_index = jnp.arange(N_ROW * N_COL * CAP, dtype=jnp.int32)
    device = slot_index // CAP
    position = tile_pos.reshape(-1).astype(jnp.int32)
    column_span = N_ROW * BLK_DEV
    local_column = position % column_span
    block_rows = device // N_COL * N_COL * BLK_DEV + position // column_span
    block_cols = (local_column // BLK_DEV * N_COL + device % N_COL) * BLK_DEV + local_column % BLK_DEV
    return (block_rows.astype(jnp.int32), block_cols.astype(jnp.int32))

def operate(vector, matrix, block_rows, block_cols, diagonal):
    blocks = vector.reshape(NRHS, BLOCKS, BLOCK_PARAMS)

    def visit(totals, slot_data):
        one_tile, row_block, col_block = slot_data
        from_cols = lax.dynamic_index_in_dim(blocks, col_block, 1, keepdims=False)
        from_rows = lax.dynamic_index_in_dim(blocks, row_block, 1, keepdims=False)
        totals = totals.at[:, row_block].add(jnp.dot(from_cols, one_tile.T, precision=highest))
        totals = totals.at[:, col_block].add(jnp.dot(from_rows, one_tile, precision=highest))
        return (totals, None)
    totals, ignored = lax.scan(visit, jnp.zeros_like(blocks), (matrix, block_rows, block_cols))
    return totals.reshape(NRHS, -1) + diagonal[None, :] * vector

def inner(first_side, second_side):
    return lax.optimization_barrier(jnp.sum(first_side * second_side, axis=1))

def reference(left_derivatives, right_derivatives, bundle_tile_slot, tile_pos, right_sides, diagonal):
    matrix = build_matrix(left_derivatives, right_derivatives, bundle_tile_slot)
    block_rows, block_cols = block_places(tile_pos)
    count_rhs = right_sides.shape[0]
    beta_now = jnp.sqrt(inner(right_sides, right_sides))
    beta_old = jnp.zeros((count_rhs,), jnp.float32)
    lanczos_old = right_sides
    lanczos_now = right_sides
    delta_bar = jnp.zeros((count_rhs,), jnp.float32)
    epsilon_now = jnp.zeros((count_rhs,), jnp.float32)
    phi_bar = beta_now
    cosine = -jnp.ones((count_rhs,), jnp.float32)
    sine_now = jnp.zeros((count_rhs,), jnp.float32)
    search_now = jnp.zeros_like(right_sides)
    search_old = jnp.zeros_like(right_sides)
    solution = jnp.zeros_like(right_sides)
    for iteration in range(ITERS):
        basis = lanczos_now / beta_now[:, None]
        image = operate(basis, matrix, block_rows, block_cols, diagonal)
        if iteration > 0:
            image = image - (beta_now / beta_old)[:, None] * lanczos_old
        alpha_now = inner(basis, image)
        image = image - (alpha_now / beta_now)[:, None] * lanczos_now
        lanczos_old, lanczos_now = (lanczos_now, image)
        beta_old, beta_now = (beta_now, jnp.sqrt(inner(image, image)))
        epsilon_old = epsilon_now
        delta_now = cosine * delta_bar + sine_now * alpha_now
        gamma_bar = sine_now * delta_bar - cosine * alpha_now
        epsilon_now = sine_now * beta_now
        delta_bar = -cosine * beta_now
        gamma_now = jnp.sqrt(gamma_bar * gamma_bar + beta_now * beta_now)
        cosine = gamma_bar / gamma_now
        sine_now = beta_now / gamma_now
        phi_now = cosine * phi_bar
        phi_bar = sine_now * phi_bar
        search_older, search_old = (search_old, search_now)
        search_now = (basis - epsilon_old[:, None] * search_older - delta_now[:, None] * search_old) / gamma_now[:, None]
        solution = solution + phi_now[:, None] * search_now
    return solution
```

```python
import jax
import jax.numpy as jnp
from jax import lax
from jax.sharding import PartitionSpec as P

ITERS = 3


def block_places(bundle_tile_slot, tile_pos, blk_dev):
    row_count, col_count = lax.axis_size("row"), lax.axis_size("col")
    cap = tile_pos.shape[-1]
    band_pos = lax.all_gather(tile_pos.reshape(-1), "col", axis=0, tiled=True)
    owner = bundle_tile_slot // cap % col_count
    position = jnp.take(band_pos, bundle_tile_slot % (cap * col_count))
    span = row_count * blk_dev
    local = position % span
    rows = lax.axis_index("row") * col_count * blk_dev + position // span
    cols = (local // blk_dev * col_count + owner) * blk_dev + local % blk_dev
    return rows, cols


def body(left_derivatives, right_derivatives, bundle_tile_slot, tile_pos, right_sides, diagonal):
    width = left_derivatives.shape[2]
    nrhs, own = right_sides.shape
    blk = own // width
    blocks = blk * lax.axis_size("row") * lax.axis_size("col")
    axes = ("row", "col")
    b = right_sides.reshape(nrhs, blk, width).transpose(1, 0, 2)
    diag = diagonal.reshape(blk, 1, width)
    gram = jnp.einsum(
        "nma,nmb->nab", left_derivatives, right_derivatives, preferred_element_type=jnp.float32
    ).astype(jnp.bfloat16)
    rows, cols = block_places(bundle_tile_slot, tile_pos, blk)
    targets = jnp.concatenate([rows, cols])
    scatter = (jnp.arange(blocks, dtype=jnp.int32)[:, None] == targets[None, :]).astype(jnp.bfloat16)

    def apply(x):
        everywhere = lax.all_gather(x.astype(jnp.bfloat16), axes, axis=0, tiled=True)
        at_rows = jnp.take(everywhere, rows, axis=0)
        at_cols = jnp.take(everywhere, cols, axis=0)
        row_terms = jnp.einsum("crb,cab->cra", at_cols, gram, preferred_element_type=jnp.float32)
        col_terms = jnp.einsum("cra,cab->crb", at_rows, gram, preferred_element_type=jnp.float32)
        terms = jnp.concatenate([row_terms, col_terms]).astype(jnp.bfloat16)
        total = jnp.einsum("kc,crp->krp", scatter, terms, preferred_element_type=jnp.float32)
        return lax.psum_scatter(
            total.astype(jnp.bfloat16), axes, scatter_dimension=0, tiled=True
        ).astype(jnp.float32)

    def sums(*terms):
        return lax.psum(jnp.stack([jnp.sum(t, axis=(0, 2)) for t in terms]), axes)

    def wide(s):
        return s[None, :, None]

    first = sums(b * b, diag * b * b)
    beta = jnp.sqrt(first[0])
    v = b / wide(beta)
    v_old = None
    sv = apply(b) / wide(beta)
    sigma = first[1] / first[0]
    zero = jnp.zeros((nrhs,), jnp.float32)
    delta_bar, eps, phi_bar = zero, zero, beta
    cs, sn = -jnp.ones((nrhs,), jnp.float32), zero
    w = w_old = out = jnp.zeros_like(b)
    for step in range(ITERS):
        y = diag * v + sv - wide(sigma) * v
        if step > 0:
            y = y - wide(beta) * v_old
        dots = sums(v * y, y * y, v * v)
        alpha = sigma * dots[2] + dots[0]
        shift = alpha - sigma
        beta_next = jnp.sqrt(
            jnp.maximum(dots[1] - 2 * shift * dots[0] + shift * shift * dots[2], 0.0)
        )
        eps_old = eps
        delta = cs * delta_bar + sn * alpha
        gamma_bar = sn * delta_bar - cs * alpha
        eps = sn * beta_next
        delta_bar = -cs * beta_next
        gamma = jnp.sqrt(gamma_bar * gamma_bar + beta_next * beta_next)
        cs = gamma_bar / gamma
        sn = beta_next / gamma
        phi = cs * phi_bar
        phi_bar = sn * phi_bar
        w_older, w_old = w_old, w
        w = (v - wide(eps_old) * w_older - wide(delta) * w_old) / wide(gamma)
        out = out + wide(phi) * w
        if step < ITERS - 1:
            z = apply(y)
            v_old = v
            sv = (z - wide(shift) * sv) / wide(beta_next)
            v = (y - wide(shift) * v) / wide(beta_next)
            beta, sigma = beta_next, alpha
    return out.transpose(1, 0, 2).reshape(nrhs, own)


def solution(mesh):
    placed = (
        P(("row", "col"), None, None),
        P(("row", "col"), None, None),
        P(("row", "col")),
        P("row", "col", None),
        P(None, ("row", "col")),
        P(("row", "col")),
    )
    return jax.shard_map(
        body, mesh=mesh, in_specs=placed, out_specs=P(None, ("row", "col")), check_vma=False
    )
```

```python
import functools

import jax
import jax.numpy as jnp
from jax import lax
from jax.experimental import pallas as pl
from jax.experimental.pallas import tpu as pltpu
from jax.sharding import PartitionSpec as P

ITERS = 3
CORES = 2
MESH = pl.DeviceIdType.MESH


class Layout:
    def __init__(self, rows, cols, blk):
        self.Y, self.C = rows // CORES, CORES
        x = 1
        while 4 * x * x <= cols:
            x *= 2
        self.X, self.Z = x, cols // x
        self.devices = rows * cols
        self.hb = blk // 2
        self.size = {"z": self.Z, "x": self.X, "y": self.Y, "core": self.C}
        self.orders = (("z", "x", "y", "core"), ("z", "y", "x", "core"))
        self.strides = []
        for order in self.orders:
            strides, run = [], 1
            for axis in order:
                strides.append(run)
                run *= self.size[axis]
            self.strides.append(strides)

    def coords(self, row, col):
        return {"z": col // self.X, "x": col % self.X, "y": row // CORES, "core": row % CORES}

    def device(self, c):
        return (c["y"] * CORES + c["core"], c["z"] * self.X + c["x"])

    def base(self, half, c, level):
        order, strides = self.orders[half], self.strides[half]
        return sum(c[order[l]] * strides[l] for l in range(level, 4))

    def block(self, row, col, m):
        c = self.coords(row, col)
        half = m // self.hb
        at = jnp.where(half == 0, self.base(0, c, 0), self.base(1, c, 0))
        return (half * self.devices + at) * self.hb + m % self.hb


def kernel(
    lay, nb, width, nrhs, blk,
    pick_ref, prev_ref, last_ref, left_hbm, right_hbm, b_ref, d_ref, out_ref,
    lbuf, rbuf, gram, xall, part, r0, r1, r2, r3, acc, dots,
    v, v_old, sv, y, w, w_old, z,
    in_sem, ag_send, ag_recv, rs_send, rs_recv,
):
    row, col = lax.axis_index("row"), lax.axis_index("col")
    me = lay.coords(row, col)
    hb = lay.hb
    half_blocks = lay.devices * hb
    recv_bufs = (r0, r1, r2, r3)

    def peer(axis, offset):
        other = dict(me)
        other[axis] = lax.rem(me[axis] + offset, lay.size[axis])
        return other

    for i in range(nb):
        pltpu.make_async_copy(left_hbm.at[i], lbuf.at[i], in_sem.at[0, i]).start()
        pltpu.make_async_copy(right_hbm.at[i], rbuf.at[i], in_sem.at[1, i]).start()

    barrier = pltpu.get_barrier_semaphore()
    greeted = 0
    for axis in ("z", "x", "y", "core"):
        for o in range(1, lay.size[axis]):
            pl.semaphore_signal(
                barrier, inc=1, device_id=lay.device(peer(axis, o)), device_id_type=MESH
            )
            greeted += 1
    pl.semaphore_wait(barrier, greeted)

    dot_axes = ("z", "x", "y", "core")
    lane = lax.broadcasted_iota(jnp.int32, (nrhs, 128), 1)

    def put_dots(*values):
        tile = jnp.zeros((nrhs, 128), jnp.float32)
        for j, value in enumerate(values):
            tile = jnp.where(lane == j, jnp.sum(value, axis=1, keepdims=True), tile)
        dots[0, me["z"]] = tile

    def start_dots(level):
        copies = []
        axis = dot_axes[level]
        for o in range(1, lay.size[axis]):
            src = dots.at[level, me[axis]]
            copy = pltpu.make_async_remote_copy(
                src_ref=src, dst_ref=src,
                send_sem=ag_send.at[2, level, o], recv_sem=ag_recv.at[2, level, o],
                device_id=lay.device(peer(axis, o)), device_id_type=MESH,
            )
            copy.start()
            copies.append(copy)
        return copies

    def sum_dots(level):
        total = dots[level, 0]
        for s in range(1, lay.size[dot_axes[level]]):
            total = total + dots[level, s]
        if level < 3:
            dots[level + 1, me[dot_axes[level + 1]]] = total
        return total

    def pick_dot(total, j):
        return jnp.sum(jnp.where(lane == j, total, 0.0), axis=1, keepdims=True)

    def gather(x_ref, hook=None):
        for m in range(blk):
            h = m // hb
            xall[h * half_blocks + lay.base(h, me, 0) * hb + m % hb] = x_ref[
                :, m * width:(m + 1) * width
            ].astype(jnp.bfloat16)
        total = None
        for level in range(4):
            copies = start_dots(level)
            for h in range(2):
                axis = lay.orders[h][level]
                run = lay.strides[h][level] * hb
                src = xall.at[pl.ds(h * half_blocks + lay.base(h, me, level) * hb, run)]
                for o in range(1, lay.size[axis]):
                    copy = pltpu.make_async_remote_copy(
                        src_ref=src, dst_ref=src,
                        send_sem=ag_send.at[h, level, o], recv_sem=ag_recv.at[h, level, o],
                        device_id=lay.device(peer(axis, o)), device_id_type=MESH,
                    )
                    copy.start()
                    copies.append(copy)
            if hook is not None:
                hook(level)
            for copy in copies:
                copy.wait()
            total = sum_dots(level)
        return total

    def reduce_dots():
        total = None
        for level in range(4):
            for copy in start_dots(level):
                copy.wait()
            total = sum_dots(level)
        return total

    def products():
        acc[2 * nb] = jnp.zeros((nrhs, width), jnp.float32)

        def one(i, carry):
            g = gram[i]
            x_row = xall[pick_ref[2 * i]]
            x_col = xall[pick_ref[2 * i + 1]]
            row_term = lax.dot_general(
                x_col, g, (((1,), (1,)), ((), ())), preferred_element_type=jnp.float32
            )
            col_term = jnp.dot(x_row, g, preferred_element_type=jnp.float32)
            acc[2 * i] = row_term + acc[prev_ref[2 * i]]
            acc[2 * i + 1] = col_term + acc[prev_ref[2 * i + 1]]
            return carry

        lax.fori_loop(0, nb, one, 0)

        def spread(k, carry):
            for u in range(4):
                part[4 * k + u] = acc[last_ref[4 * k + u]].astype(jnp.bfloat16)
            return carry

        lax.fori_loop(0, 2 * half_blocks // 4, spread, 0)

    def scatter_sum():
        for level in (3, 2, 1, 0):
            copies = []
            for h in range(2):
                axis = lay.orders[h][level]
                run = lay.strides[h][level] * hb
                for o in range(1, lay.size[axis]):
                    other = peer(axis, o)
                    at = dict(me)
                    at[axis] = other[axis]
                    copy = pltpu.make_async_remote_copy(
                        src_ref=part.at[pl.ds(h * half_blocks + lay.base(h, at, level) * hb, run)],
                        dst_ref=recv_bufs[level].at[h, o - 1, pl.ds(0, run)],
                        send_sem=rs_send.at[h, level, o], recv_sem=rs_recv.at[h, level, o],
                        device_id=lay.device(other), device_id_type=MESH,
                    )
                    copy.start()
                    copies.append(copy)
            for copy in copies:
                copy.wait()
            for h in range(2):
                axis = lay.orders[h][level]
                run = lay.strides[h][level] * hb
                start = h * half_blocks + lay.base(h, me, level) * hb

                def total(i):
                    value = part[start + i].astype(jnp.float32)
                    for o in range(1, lay.size[axis]):
                        value = value + recv_bufs[level][h, o - 1, i].astype(jnp.float32)
                    return value

                if level == 0:
                    for i in range(hb):
                        m = h * hb + i
                        z[:, m * width:(m + 1) * width] = total(i)
                else:

                    def add(i, carry):
                        for u in range(2):
                            part[start + 2 * i + u] = total(2 * i + u).astype(jnp.bfloat16)
                        return carry

                    lax.fori_loop(0, run // 2, add, 0)

    def make_grams(level):
        def one(i, carry):
            pltpu.make_async_copy(left_hbm.at[i], lbuf.at[i], in_sem.at[0, i]).wait()
            pltpu.make_async_copy(right_hbm.at[i], rbuf.at[i], in_sem.at[1, i]).wait()
            gram[i] = lax.dot_general(
                lbuf[i], rbuf[i], (((0,), (0,)), ((), ())), preferred_element_type=jnp.float32
            ).astype(jnp.bfloat16)
            return carry

        lax.fori_loop(level * nb // 4, (level + 1) * nb // 4, one, 0)

    b = b_ref[...]
    put_dots(b * b, d_ref[...] * b * b)
    total = gather(b_ref, make_grams)
    first = pick_dot(total, 0)
    beta = jnp.sqrt(first)
    sigma = pick_dot(total, 1) / first
    products()
    scatter_sum()
    v[...] = b_ref[...] / beta
    sv[...] = z[...] / beta
    zero = jnp.zeros_like(beta)
    delta_bar, eps, phi_bar = zero, zero, beta
    cs, sn = -jnp.ones_like(beta), zero
    for step in range(ITERS):
        vv = v[...]
        value = d_ref[...] * vv + sv[...] - sigma * vv
        if step > 0:
            value = value - beta * v_old[...]
        y[...] = value
        put_dots(vv * value, value * value, vv * vv)
        total = gather(y) if step < ITERS - 1 else reduce_dots()
        vy, yy, ones = pick_dot(total, 0), pick_dot(total, 1), pick_dot(total, 2)
        alpha = sigma * ones + vy
        shift = alpha - sigma
        beta_next = jnp.sqrt(jnp.maximum(yy - 2 * shift * vy + shift * shift * ones, 0.0))
        eps_old = eps
        delta = cs * delta_bar + sn * alpha
        gamma_bar = sn * delta_bar - cs * alpha
        eps = sn * beta_next
        delta_bar = -cs * beta_next
        gamma = jnp.sqrt(gamma_bar * gamma_bar + beta_next * beta_next)
        cs = gamma_bar / gamma
        sn = beta_next / gamma
        phi = cs * phi_bar
        phi_bar = sn * phi_bar
        search = v[...]
        if step > 1:
            search = search - eps_old * w_old[...]
        if step > 0:
            search = search - delta * w[...]
            w_old[...] = w[...]
        search = search / gamma
        w[...] = search
        if step == 0:
            out_ref[...] = phi * search
            w_old[...] = jnp.zeros_like(search)
        else:
            out_ref[...] = out_ref[...] + phi * search
        if step < ITERS - 1:
            products()
            scatter_sum()
            v_old[...] = v[...]
            sv[...] = (z[...] - shift * sv[...]) / beta_next
            v[...] = (y[...] - shift * v[...]) / beta_next
            beta, sigma = beta_next, alpha


def body(rows, cols, left, right, bundle_tile_slot, tile_pos, right_sides, diagonal):
    nb, measures, width = left.shape
    nrhs, own = right_sides.shape
    blk = own // width
    lay = Layout(rows, cols, blk)
    cap = tile_pos.shape[-1]
    band_pos = lax.all_gather(tile_pos.reshape(-1), "col", axis=0, tiled=True)
    owner = bundle_tile_slot // cap % cols
    wanted = bundle_tile_slot % (cap * cols)
    hit = wanted[:, None] == jnp.arange(cap * cols, dtype=jnp.int32)[None, :]
    position = jnp.sum(jnp.where(hit, band_pos[None, :], 0), axis=1)
    span = rows * blk
    row_block, local = position // span, position % span
    at_row = lay.block(lax.axis_index("row"), row_block // blk, row_block % blk)
    at_col = lay.block(local // blk, owner, local % blk)
    target = jnp.stack([at_row, at_col], axis=1).reshape(-1)
    number = jnp.arange(2 * nb, dtype=jnp.int32)
    same = (target[:, None] == target[None, :]) & (number[None, :] < number[:, None])
    prev = jnp.max(jnp.where(same, number[None, :], -1), axis=1)
    prev = jnp.where(prev < 0, 2 * nb, prev)
    blocks = blk * rows * cols
    found = target[None, :] == jnp.arange(blocks, dtype=jnp.int32)[:, None]
    last = jnp.max(jnp.where(found, number[None, :], -1), axis=1)
    last = jnp.where(last < 0, 2 * nb, last)

    hb = lay.hb
    bf16, f32 = jnp.bfloat16, jnp.float32
    most = max(lay.size.values())

    def landing(level):
        peers = max(lay.size[order[level]] for order in lay.orders) - 1
        run = max(strides[level] for strides in lay.strides) * hb
        return pltpu.VMEM((2, max(peers, 1), run, nrhs, width), bf16)

    smem = pl.BlockSpec(memory_space=pltpu.SMEM)
    vmem = pl.BlockSpec(memory_space=pltpu.VMEM)
    hbm = pl.BlockSpec(memory_space=pl.ANY)
    state = pltpu.VMEM((nrhs, own), f32)
    return pl.pallas_call(
        functools.partial(kernel, lay, nb, width, nrhs, blk),
        out_shape=jax.ShapeDtypeStruct((nrhs, own), f32),
        in_specs=[smem, smem, smem, hbm, hbm, vmem, vmem],
        out_specs=vmem,
        scratch_shapes=[
            pltpu.VMEM((nb, measures, width), bf16),
            pltpu.VMEM((nb, measures, width), bf16),
            pltpu.VMEM((nb, width, width), bf16),
            pltpu.VMEM((blocks, nrhs, width), bf16),
            pltpu.VMEM((blocks, nrhs, width), bf16),
            landing(0), landing(1), landing(2), landing(3),
            pltpu.VMEM((2 * nb + 1, nrhs, width), f32),
            pltpu.VMEM((4, most, nrhs, 128), f32),
            state, state, state, state, state, state, state,
            pltpu.SemaphoreType.DMA((2, nb)),
            pltpu.SemaphoreType.DMA((3, 4, most)),
            pltpu.SemaphoreType.DMA((3, 4, most)),
            pltpu.SemaphoreType.DMA((2, 4, most)),
            pltpu.SemaphoreType.DMA((2, 4, most)),
        ],
        compiler_params=pltpu.CompilerParams(
            collective_id=0, has_side_effects=True, vmem_limit_bytes=60 * 1024 * 1024
        ),
    )(target, prev, last, left, right, right_sides, diagonal.reshape(1, own))


def solution(mesh):
    placed = (
        P(("row", "col"), None, None),
        P(("row", "col"), None, None),
        P(("row", "col")),
        P("row", "col", None),
        P(None, ("row", "col")),
        P(("row", "col")),
    )
    return jax.shard_map(
        functools.partial(body, mesh.shape["row"], mesh.shape["col"]),
        mesh=mesh, in_specs=placed, out_specs=P(None, ("row", "col")), check_vma=False,
    )
```

```python
import functools

import jax
import jax.numpy as jnp
from jax import lax
from jax.experimental import pallas as pl
from jax.experimental.pallas import tpu as pltpu
from jax.sharding import PartitionSpec as P

ITERS = 3
CORES = 2
MESH = pl.DeviceIdType.MESH


class Layout:
    def __init__(self, rows, cols, blk):
        self.Y, self.C = rows // CORES, CORES
        x = 1
        while 4 * x * x <= cols:
            x *= 2
        self.X, self.Z = x, cols // x
        self.devices = rows * cols
        self.hb = blk // 2
        self.size = {"z": self.Z, "x": self.X, "y": self.Y, "core": self.C}
        self.orders = (("x", "y"), ("y", "x"))

    def coords(self, row, col):
        return {"z": col // self.X, "x": col % self.X, "y": row // CORES, "core": row % CORES}

    def device(self, c):
        return (c["y"] * CORES + c["core"], c["z"] * self.X + c["x"])

    def chunk(self, half, c):
        near, far = self.orders[half]
        at = c["core"] * self.Z + c["z"]
        return (at * self.size[far] + c[far]) * self.size[near] + c[near]

    def block(self, row, col, m):
        c = self.coords(row, col)
        half = m // self.hb
        at = jnp.where(half == 0, self.chunk(0, c), self.chunk(1, c))
        return (half * self.devices + at) * self.hb + m % self.hb


def kernel(
    lay, nb, width, nrhs, blk,
    pick_ref, prev_ref, last_ref, left_hbm, right_hbm, b_ref, d_ref, out_ref,
    lbuf, rbuf, gram, xall, part, r_z, r_near, r_far, r_core, acc, dots,
    v, v_old, sv, y, w, w_old, z,
    in_sem, dot_send, dot_recv, *sems,
):
    row, col = lax.axis_index("row"), lax.axis_index("col")
    me = lay.coords(row, col)
    hb = lay.hb
    half_blocks = lay.devices * hb
    ag_z, ag_near, ag_far, ag_core = [sems[i:i + 2] for i in range(0, 8, 2)]
    rs_z, rs_near, rs_far, rs_core = [sems[i:i + 2] for i in range(8, 16, 2)]

    def peer(axis, offset):
        other = dict(me)
        other[axis] = lax.rem(me[axis] + offset, lay.size[axis])
        return other

    for i in range(nb):
        pltpu.make_async_copy(left_hbm.at[i], lbuf.at[i], in_sem.at[0, i]).start()
        pltpu.make_async_copy(right_hbm.at[i], rbuf.at[i], in_sem.at[1, i]).start()

    barrier = pltpu.get_barrier_semaphore()
    greeted = 0
    for axis in ("z", "x", "y", "core"):
        for o in range(1, lay.size[axis]):
            pl.semaphore_signal(
                barrier, inc=1, device_id=lay.device(peer(axis, o)), device_id_type=MESH
            )
            greeted += 1
    pl.semaphore_wait(barrier, greeted)

    dot_axes = ("z", "x", "y", "core")
    lane = lax.broadcasted_iota(jnp.int32, (nrhs, 128), 1)

    def put_dots(*values):
        tile = jnp.zeros((nrhs, 128), jnp.float32)
        for j, value in enumerate(values):
            tile = jnp.where(lane == j, jnp.sum(value, axis=1, keepdims=True), tile)
        dots[0, me["z"]] = tile

    def start_dots(level):
        copies = []
        axis = dot_axes[level]
        for o in range(1, lay.size[axis]):
            src = dots.at[level, me[axis]]
            copy = pltpu.make_async_remote_copy(
                src_ref=src, dst_ref=src,
                send_sem=dot_send.at[level, o], recv_sem=dot_recv.at[level, o],
                device_id=lay.device(peer(axis, o)), device_id_type=MESH,
            )
            copy.start()
            copies.append(copy)
        return copies

    def sum_dots(level):
        total = dots[level, 0]
        for s in range(1, lay.size[dot_axes[level]]):
            total = total + dots[level, s]
        if level < 3:
            dots[level + 1, me[dot_axes[level + 1]]] = total
        return total

    def pick_dot(total, j):
        return jnp.sum(jnp.where(lane == j, total, 0.0), axis=1, keepdims=True)

    def place(h, oz=0, o1=0, o2=0, other_core=False):
        near, far = lay.orders[h]
        c = dict(me)
        for axis, o in (("z", oz), (near, o1), (far, o2)):
            if o:
                c[axis] = lax.rem(me[axis] + o, lay.size[axis])
        if other_core:
            c["core"] = 1 - me["core"]
        return h * half_blocks + lay.chunk(h, c) * hb

    def group(h, oz, other_core=False):
        c = dict(me, z=lax.rem(me["z"] + oz, lay.Z), x=0, y=0)
        if other_core:
            c["core"] = 1 - me["core"]
        return h * half_blocks + lay.chunk(h, c) * hb

    def send(src, dst, sems, index, other):
        copy = pltpu.make_async_remote_copy(
            src_ref=src, dst_ref=dst, send_sem=sems[0].at[index], recv_sem=sems[1].at[index],
            device_id=lay.device(other), device_id_type=MESH,
        )
        copy.start()
        return copy

    spans = [[lay.size[axis] for axis in order] for order in lay.orders]
    run = lay.X * lay.Y * hb
    z_near_first = sorted(range(1, lay.Z), key=lambda o: (min(o, lay.Z - o), o))

    def gather(x_ref, hook=None):
        for m in range(blk):
            h = m // hb
            xall[place(h) + m % hb] = x_ref[:, m * width:(m + 1) * width].astype(jnp.bfloat16)
        sent = []

        def push(at, count, sems, index, other):
            ref = xall.at[pl.ds(at, count)]
            copy = send(ref, ref, sems, index, other)
            sent.append(copy)
            return copy

        small = start_dots(0)
        by_z, by_near, by_far, by_core = {}, {}, {}, []
        for o in z_near_first:
            for h in range(2):
                by_z[h, o] = push(place(h), hb, ag_z, (h, o), peer("z", o))
        order = [0] + z_near_first
        slots = len(order)
        for t in range(slots + 2):
            if t < slots:
                o = order[t]
                oz = (lay.Z - o) % lay.Z
                for h in range(2):
                    if o:
                        by_z[h, o].wait_recv()
                    near, far = lay.orders[h]
                    for o1 in range(1, spans[h][0]):
                        by_near[h, oz, o1] = push(
                            place(h, oz), hb, ag_near, (h, oz, o1), peer(near, o1)
                        )
                    for o2 in range(1, spans[h][1]):
                        by_far[h, oz, 0, o2] = push(
                            place(h, oz), hb, ag_far, (h, oz, 0, o2), peer(far, o2)
                        )
            if 1 <= t <= slots:
                oz = (lay.Z - order[t - 1]) % lay.Z
                for h in range(2):
                    near, far = lay.orders[h]
                    for o1 in range(1, spans[h][0]):
                        by_near[h, oz, o1].wait_recv()
                        back = spans[h][0] - o1
                        for o2 in range(1, spans[h][1]):
                            by_far[h, oz, back, o2] = push(
                                place(h, oz, back), hb, ag_far, (h, oz, back, o2), peer(far, o2)
                            )
            if t >= 2:
                oz = (lay.Z - order[t - 2]) % lay.Z
                for h in range(2):
                    for o1 in range(spans[h][0]):
                        for o2 in range(1, spans[h][1]):
                            by_far[h, oz, o1, o2].wait_recv()
                    by_core.append(push(group(h, oz), run, ag_core, (h, oz), peer("core", 1)))
            if hook is not None and t < 4:
                hook(t)
            level = {slots - 1: 0, slots: 1, slots + 1: 2}.get(t)
            if level is not None:
                for copy in small:
                    copy.wait()
                sum_dots(level)
                small = start_dots(level + 1)
        for copy in by_core:
            copy.wait_recv()
        for copy in sent:
            copy.wait_send()
        for copy in small:
            copy.wait()
        return sum_dots(3)

    def reduce_dots():
        total = None
        for level in range(4):
            for copy in start_dots(level):
                copy.wait()
            total = sum_dots(level)
        return total

    def products():
        acc[2 * nb] = jnp.zeros((nrhs, width), jnp.float32)

        def one(i, carry):
            g = gram[i]
            x_row = xall[pick_ref[2 * i]]
            x_col = xall[pick_ref[2 * i + 1]]
            row_term = lax.dot_general(
                x_col, g, (((1,), (1,)), ((), ())), preferred_element_type=jnp.float32
            )
            col_term = jnp.dot(x_row, g, preferred_element_type=jnp.float32)
            acc[2 * i] = row_term + acc[prev_ref[2 * i]]
            acc[2 * i + 1] = col_term + acc[prev_ref[2 * i + 1]]
            return carry

        lax.fori_loop(0, nb, one, 0)

    def scatter_sum():
        sent = []
        z_far_first = z_near_first[::-1] + [0]
        by_core, by_far, by_near, by_z = {}, {}, {}, {}
        for oz in z_far_first:
            for h in range(2):
                at = group(h, oz, True)

                def spread(i, carry):
                    for u in range(2):
                        k = at + 2 * i + u
                        part[k] = acc[last_ref[k]].astype(jnp.bfloat16)
                    return carry

                lax.fori_loop(0, run // 2, spread, 0)
                by_core[h, oz] = send(
                    part.at[pl.ds(at, run)], r_core.at[h, oz], rs_core, (h, oz), peer("core", 1)
                )
                sent.append(by_core[h, oz])

        def total(h, oz, o1, o2, i):
            at = place(h, oz, o1, o2) + i
            value = acc[last_ref[at]] + r_core[h, oz, at - group(h, oz)].astype(jnp.float32)
            if o2 == 0:
                for o in range(1, spans[h][1]):
                    value = value + r_far[h, oz, o1, o - 1, i].astype(jnp.float32)
                if o1 == 0:
                    for o in range(1, spans[h][0]):
                        value = value + r_near[h, oz, o - 1, i].astype(jnp.float32)
                    if oz == 0:
                        for o in range(1, lay.Z):
                            value = value + r_z[h, o - 1, i].astype(jnp.float32)
            return value

        def forward(h, oz, o1, o2, dst, sems, index, other):
            at = place(h, oz, o1, o2)
            for i in range(hb):
                part[at + i] = total(h, oz, o1, o2, i).astype(jnp.bfloat16)
            copy = send(part.at[pl.ds(at, hb)], dst, sems, index, other)
            sent.append(copy)
            return copy

        slots = len(z_far_first)
        for t in range(slots + 2):
            if t < slots:
                oz = z_far_first[t]
                for h in range(2):
                    near, far = lay.orders[h]
                    by_core[h, oz].wait_recv()
                    for o1 in list(range(1, spans[h][0])) + [0]:
                        for o2 in range(1, spans[h][1]):
                            by_far[h, oz, o1, o2] = forward(
                                h, oz, o1, o2, r_far.at[h, oz, o1, o2 - 1],
                                rs_far, (h, oz, o1, o2), peer(far, o2),
                            )
            if 1 <= t <= slots:
                oz = z_far_first[t - 1]
                for h in range(2):
                    near, far = lay.orders[h]
                    for o1 in range(1, spans[h][0]):
                        for o2 in range(1, spans[h][1]):
                            by_far[h, oz, o1, o2].wait_recv()
                        by_near[h, oz, o1] = forward(
                            h, oz, o1, 0, r_near.at[h, oz, o1 - 1],
                            rs_near, (h, oz, o1), peer(near, o1),
                        )
            if t >= 2:
                oz = z_far_first[t - 2]
                for h in range(2):
                    for o2 in range(1, spans[h][1]):
                        by_far[h, oz, 0, o2].wait_recv()
                    for o1 in range(1, spans[h][0]):
                        by_near[h, oz, o1].wait_recv()
                    if oz:
                        by_z[h, oz] = forward(
                            h, oz, 0, 0, r_z.at[h, oz - 1], rs_z, (h, oz), peer("z", oz)
                        )
        for h in range(2):
            for o in range(1, lay.Z):
                by_z[h, o].wait_recv()
            for i in range(hb):
                m = h * hb + i
                z[:, m * width:(m + 1) * width] = total(h, 0, 0, 0, i)
        for copy in sent:
            copy.wait_send()

    def make_grams(level):
        def one(i, carry):
            pltpu.make_async_copy(left_hbm.at[i], lbuf.at[i], in_sem.at[0, i]).wait()
            pltpu.make_async_copy(right_hbm.at[i], rbuf.at[i], in_sem.at[1, i]).wait()
            gram[i] = lax.dot_general(
                lbuf[i], rbuf[i], (((0,), (0,)), ((), ())), preferred_element_type=jnp.float32
            ).astype(jnp.bfloat16)
            return carry

        lax.fori_loop(level * nb // 4, (level + 1) * nb // 4, one, 0)

    b = b_ref[...]
    put_dots(b * b, d_ref[...] * b * b)
    total = gather(b_ref, make_grams)
    first = pick_dot(total, 0)
    beta = jnp.sqrt(first)
    sigma = pick_dot(total, 1) / first
    products()
    scatter_sum()
    v[...] = b_ref[...] / beta
    sv[...] = z[...] / beta
    zero = jnp.zeros_like(beta)
    delta_bar, eps, phi_bar = zero, zero, beta
    cs, sn = -jnp.ones_like(beta), zero
    for step in range(ITERS):
        vv = v[...]
        value = d_ref[...] * vv + sv[...] - sigma * vv
        if step > 0:
            value = value - beta * v_old[...]
        y[...] = value
        put_dots(vv * value, value * value, vv * vv)
        total = gather(y) if step < ITERS - 1 else reduce_dots()
        vy, yy, ones = pick_dot(total, 0), pick_dot(total, 1), pick_dot(total, 2)
        alpha = sigma * ones + vy
        shift = alpha - sigma
        beta_next = jnp.sqrt(jnp.maximum(yy - 2 * shift * vy + shift * shift * ones, 0.0))
        eps_old = eps
        delta = cs * delta_bar + sn * alpha
        gamma_bar = sn * delta_bar - cs * alpha
        eps = sn * beta_next
        delta_bar = -cs * beta_next
        gamma = jnp.sqrt(gamma_bar * gamma_bar + beta_next * beta_next)
        cs = gamma_bar / gamma
        sn = beta_next / gamma
        phi = cs * phi_bar
        phi_bar = sn * phi_bar
        search = v[...]
        if step > 1:
            search = search - eps_old * w_old[...]
        if step > 0:
            search = search - delta * w[...]
            w_old[...] = w[...]
        search = search / gamma
        w[...] = search
        if step == 0:
            out_ref[...] = phi * search
            w_old[...] = jnp.zeros_like(search)
        else:
            out_ref[...] = out_ref[...] + phi * search
        if step < ITERS - 1:
            products()
            scatter_sum()
            v_old[...] = v[...]
            sv[...] = (z[...] - shift * sv[...]) / beta_next
            v[...] = (y[...] - shift * v[...]) / beta_next
            beta, sigma = beta_next, alpha


def body(rows, cols, left, right, bundle_tile_slot, tile_pos, right_sides, diagonal):
    nb, measures, width = left.shape
    nrhs, own = right_sides.shape
    blk = own // width
    lay = Layout(rows, cols, blk)
    cap = tile_pos.shape[-1]
    band_pos = lax.all_gather(tile_pos.reshape(-1), "col", axis=0, tiled=True)
    owner = bundle_tile_slot // cap % cols
    wanted = bundle_tile_slot % (cap * cols)
    hit = wanted[:, None] == jnp.arange(cap * cols, dtype=jnp.int32)[None, :]
    position = jnp.sum(jnp.where(hit, band_pos[None, :], 0), axis=1)
    span = rows * blk
    row_block, local = position // span, position % span
    at_row = lay.block(lax.axis_index("row"), row_block // blk, row_block % blk)
    at_col = lay.block(local // blk, owner, local % blk)
    target = jnp.stack([at_row, at_col], axis=1).reshape(-1)
    number = jnp.arange(2 * nb, dtype=jnp.int32)
    same = (target[:, None] == target[None, :]) & (number[None, :] < number[:, None])
    prev = jnp.max(jnp.where(same, number[None, :], -1), axis=1)
    prev = jnp.where(prev < 0, 2 * nb, prev)
    blocks = blk * rows * cols
    found = target[None, :] == jnp.arange(blocks, dtype=jnp.int32)[:, None]
    last = jnp.max(jnp.where(found, number[None, :], -1), axis=1)
    last = jnp.where(last < 0, 2 * nb, last)

    hb = lay.hb
    bf16, f32 = jnp.bfloat16, jnp.float32
    most = max(lay.size.values())

    wide = max(lay.X, lay.Y)
    runs = lay.X * lay.Y * hb

    def landing(*shape):
        return pltpu.VMEM((2, *shape, nrhs, width), bf16)

    counts = ((2, lay.Z), (2, lay.Z, wide), (2, lay.Z, wide, wide), (2, lay.Z))
    sems = [pltpu.SemaphoreType.DMA(shape) for shape in counts for _ in range(2)] * 2
    smem = pl.BlockSpec(memory_space=pltpu.SMEM)
    vmem = pl.BlockSpec(memory_space=pltpu.VMEM)
    hbm = pl.BlockSpec(memory_space=pl.ANY)
    state = pltpu.VMEM((nrhs, own), f32)
    return pl.pallas_call(
        functools.partial(kernel, lay, nb, width, nrhs, blk),
        out_shape=jax.ShapeDtypeStruct((nrhs, own), f32),
        in_specs=[smem, smem, smem, hbm, hbm, vmem, vmem],
        out_specs=vmem,
        scratch_shapes=[
            pltpu.VMEM((nb, measures, width), bf16),
            pltpu.VMEM((nb, measures, width), bf16),
            pltpu.VMEM((nb, width, width), bf16),
            pltpu.VMEM((blocks, nrhs, width), bf16),
            pltpu.VMEM((blocks, nrhs, width), bf16),
            landing(lay.Z - 1, hb),
            landing(lay.Z, max(wide - 1, 1), hb),
            landing(lay.Z, wide, max(wide - 1, 1), hb),
            landing(lay.Z, runs),
            pltpu.VMEM((2 * nb + 1, nrhs, width), f32),
            pltpu.VMEM((4, most, nrhs, 128), f32),
            state, state, state, state, state, state, state,
            pltpu.SemaphoreType.DMA((2, nb)),
            pltpu.SemaphoreType.DMA((4, most)),
            pltpu.SemaphoreType.DMA((4, most)),
            *sems,
        ],
        compiler_params=pltpu.CompilerParams(
            collective_id=0, has_side_effects=True, vmem_limit_bytes=60 * 1024 * 1024
        ),
    )(target, prev, last, left, right, right_sides, diagonal.reshape(1, own))


def solution(mesh):
    placed = (
        P(("row", "col"), None, None),
        P(("row", "col"), None, None),
        P(("row", "col")),
        P("row", "col", None),
        P(None, ("row", "col")),
        P(("row", "col")),
    )
    return jax.shard_map(
        functools.partial(body, mesh.shape["row"], mesh.shape["col"]),
        mesh=mesh, in_specs=placed, out_specs=P(None, ("row", "col")), check_vma=False,
    )
```

```python
import functools

import jax
import jax.numpy as jnp
from jax import lax
from jax.experimental import pallas as pl
from jax.experimental.pallas import tpu as pltpu
from jax.sharding import PartitionSpec as P

ITERS = 3
CORES = 2
MESH = pl.DeviceIdType.MESH


class Layout:
    def __init__(self, rows, cols, blk):
        self.Y, self.C = rows // CORES, CORES
        x = 1
        while 4 * x * x <= cols:
            x *= 2
        self.X, self.Z = x, cols // x
        self.devices = rows * cols
        self.hb = blk // 2
        self.size = {"z": self.Z, "x": self.X, "y": self.Y, "core": self.C}
        self.orders = (("x", "y"), ("y", "x"))

    def coords(self, row, col):
        return {"z": col // self.X, "x": col % self.X, "y": row // CORES, "core": row % CORES}

    def device(self, c):
        return (c["y"] * CORES + c["core"], c["z"] * self.X + c["x"])

    def chunk(self, half, c):
        near, far = self.orders[half]
        at = c["core"] * self.Z + c["z"]
        return (at * self.size[far] + c[far]) * self.size[near] + c[near]

    def block(self, row, col, m):
        c = self.coords(row, col)
        half = m // self.hb
        at = jnp.where(half == 0, self.chunk(0, c), self.chunk(1, c))
        return (half * self.devices + at) * self.hb + m % self.hb


def kernel(
    lay, nb, width, nrhs, blk, cap,
    slot_ref, tile_ref, left_hbm, right_hbm, b_ref, d_ref, out_ref,
    lbuf, rbuf, gram, xall, part, r_z, r_near, r_far, r_core, acc, dots,
    v, v_old, sv, y, w, w_old, z,
    tiles, tiles_s, last_v, last_ref, pick_ref, prev_ref,
    in_sem, dot_send, dot_recv, tile_send, tile_recv, local_sem, *sems,
):
    row, col = lax.axis_index("row"), lax.axis_index("col")
    me = lay.coords(row, col)
    hb = lay.hb
    half_blocks = lay.devices * hb
    ag_z, ag_near, ag_far, ag_core = [sems[i:i + 2] for i in range(0, 8, 2)]
    rs_z, rs_near, rs_far, rs_core = [sems[i:i + 2] for i in range(8, 16, 2)]

    def peer(axis, offset):
        other = dict(me)
        other[axis] = lax.rem(me[axis] + offset, lay.size[axis])
        return other

    for i in range(nb):
        pltpu.make_async_copy(left_hbm.at[i], lbuf.at[i], in_sem.at[0, i]).start()
        pltpu.make_async_copy(right_hbm.at[i], rbuf.at[i], in_sem.at[1, i]).start()

    barrier = pltpu.get_barrier_semaphore()
    greeted = 0
    for axis in ("z", "x", "y", "core"):
        for o in range(1, lay.size[axis]):
            pl.semaphore_signal(
                barrier, inc=1, device_id=lay.device(peer(axis, o)), device_id_type=MESH
            )
            greeted += 1
    pl.semaphore_wait(barrier, greeted)

    dot_axes = ("z", "x", "y", "core")
    lane = lax.broadcasted_iota(jnp.int32, (nrhs, 128), 1)

    def put_dots(*values):
        tile = jnp.zeros((nrhs, 128), jnp.float32)
        for j, value in enumerate(values):
            tile = jnp.where(lane == j, jnp.sum(value, axis=1, keepdims=True), tile)
        dots[0, me["z"]] = tile

    def start_dots(level):
        copies = []
        axis = dot_axes[level]
        for o in range(1, lay.size[axis]):
            src = dots.at[level, me[axis]]
            copy = pltpu.make_async_remote_copy(
                src_ref=src, dst_ref=src,
                send_sem=dot_send.at[level, o], recv_sem=dot_recv.at[level, o],
                device_id=lay.device(peer(axis, o)), device_id_type=MESH,
            )
            copy.start()
            copies.append(copy)
        return copies

    def sum_dots(level):
        total = dots[level, 0]
        for s in range(1, lay.size[dot_axes[level]]):
            total = total + dots[level, s]
        if level < 3:
            dots[level + 1, me[dot_axes[level + 1]]] = total
        return total

    def pick_dot(total, j):
        return jnp.sum(jnp.where(lane == j, total, 0.0), axis=1, keepdims=True)

    def place(h, oz=0, o1=0, o2=0, other_core=False):
        near, far = lay.orders[h]
        c = dict(me)
        for axis, o in (("z", oz), (near, o1), (far, o2)):
            if o:
                c[axis] = lax.rem(me[axis] + o, lay.size[axis])
        if other_core:
            c["core"] = 1 - me["core"]
        return h * half_blocks + lay.chunk(h, c) * hb

    def group(h, oz, other_core=False):
        c = dict(me, z=lax.rem(me["z"] + oz, lay.Z), x=0, y=0)
        if other_core:
            c["core"] = 1 - me["core"]
        return h * half_blocks + lay.chunk(h, c) * hb

    def send(src, dst, sems, index, other):
        copy = pltpu.make_async_remote_copy(
            src_ref=src, dst_ref=dst, send_sem=sems[0].at[index], recv_sem=sems[1].at[index],
            device_id=lay.device(other), device_id_type=MESH,
        )
        copy.start()
        return copy

    spans = [[lay.size[axis] for axis in order] for order in lay.orders]
    run = lay.X * lay.Y * hb
    z_near_first = sorted(range(1, lay.Z), key=lambda o: (min(o, lay.Z - o), o))

    def gather(x_ref, hook=None):
        for m in range(blk):
            h = m // hb
            xall[place(h) + m % hb] = x_ref[:, m * width:(m + 1) * width].astype(jnp.bfloat16)
        sent = []

        def push(at, count, sems, index, other):
            ref = xall.at[pl.ds(at, count)]
            copy = send(ref, ref, sems, index, other)
            sent.append(copy)
            return copy

        small = start_dots(0)
        by_z, by_near, by_far, by_core = {}, {}, {}, []
        for o in z_near_first:
            for h in range(2):
                by_z[h, o] = push(place(h), hb, ag_z, (h, o), peer("z", o))
        order = [0] + z_near_first
        slots = len(order)
        for t in range(slots + 2):
            if t < slots:
                o = order[t]
                oz = (lay.Z - o) % lay.Z
                for h in range(2):
                    if o:
                        by_z[h, o].wait_recv()
                    near, far = lay.orders[h]
                    for o1 in range(1, spans[h][0]):
                        by_near[h, oz, o1] = push(
                            place(h, oz), hb, ag_near, (h, oz, o1), peer(near, o1)
                        )
                    for o2 in range(1, spans[h][1]):
                        by_far[h, oz, 0, o2] = push(
                            place(h, oz), hb, ag_far, (h, oz, 0, o2), peer(far, o2)
                        )
            if 1 <= t <= slots:
                oz = (lay.Z - order[t - 1]) % lay.Z
                for h in range(2):
                    near, far = lay.orders[h]
                    for o1 in range(1, spans[h][0]):
                        by_near[h, oz, o1].wait_recv()
                        back = spans[h][0] - o1
                        for o2 in range(1, spans[h][1]):
                            by_far[h, oz, back, o2] = push(
                                place(h, oz, back), hb, ag_far, (h, oz, back, o2), peer(far, o2)
                            )
            if t >= 2:
                oz = (lay.Z - order[t - 2]) % lay.Z
                for h in range(2):
                    for o1 in range(spans[h][0]):
                        for o2 in range(1, spans[h][1]):
                            by_far[h, oz, o1, o2].wait_recv()
                    by_core.append(push(group(h, oz), run, ag_core, (h, oz), peer("core", 1)))
            if hook is not None:
                hook(t)
            level = {slots - 1: 0, slots: 1, slots + 1: 2}.get(t)
            if level is not None:
                for copy in small:
                    copy.wait()
                sum_dots(level)
                small = start_dots(level + 1)
        for copy in by_core:
            copy.wait_recv()
        for copy in sent:
            copy.wait_send()
        for copy in small:
            copy.wait()
        return sum_dots(3)

    def reduce_dots():
        total = None
        for level in range(4):
            for copy in start_dots(level):
                copy.wait()
            total = sum_dots(level)
        return total

    def products():
        acc[2 * nb] = jnp.zeros((nrhs, width), jnp.float32)

        def one(i, carry):
            g = gram[i]
            x_row = xall[pick_ref[2 * i]]
            x_col = xall[pick_ref[2 * i + 1]]
            row_term = lax.dot_general(
                x_col, g, (((1,), (1,)), ((), ())), preferred_element_type=jnp.float32
            )
            col_term = jnp.dot(x_row, g, preferred_element_type=jnp.float32)
            acc[2 * i] = row_term + acc[prev_ref[2 * i]]
            acc[2 * i + 1] = col_term + acc[prev_ref[2 * i + 1]]
            return carry

        lax.fori_loop(0, nb, one, 0)

    def scatter_sum():
        sent = []
        z_far_first = z_near_first[::-1] + [0]
        by_core, by_far, by_near, by_z = {}, {}, {}, {}
        for oz in z_far_first:
            for h in range(2):
                at = group(h, oz, True)

                def spread(i, carry):
                    for u in range(2):
                        k = at + 2 * i + u
                        part[k] = acc[last_ref[0, k]].astype(jnp.bfloat16)
                    return carry

                lax.fori_loop(0, run // 2, spread, 0)
                by_core[h, oz] = send(
                    part.at[pl.ds(at, run)], r_core.at[h, oz], rs_core, (h, oz), peer("core", 1)
                )
                sent.append(by_core[h, oz])

        def total(h, oz, o1, o2, i):
            at = place(h, oz, o1, o2) + i
            value = acc[last_ref[0, at]] + r_core[h, oz, at - group(h, oz)].astype(jnp.float32)
            if o2 == 0:
                for o in range(1, spans[h][1]):
                    value = value + r_far[h, oz, o1, o - 1, i].astype(jnp.float32)
                if o1 == 0:
                    for o in range(1, spans[h][0]):
                        value = value + r_near[h, oz, o - 1, i].astype(jnp.float32)
                    if oz == 0:
                        for o in range(1, lay.Z):
                            value = value + r_z[h, o - 1, i].astype(jnp.float32)
            return value

        def forward(h, oz, o1, o2, dst, sems, index, other):
            at = place(h, oz, o1, o2)
            for i in range(hb):
                part[at + i] = total(h, oz, o1, o2, i).astype(jnp.bfloat16)
            copy = send(part.at[pl.ds(at, hb)], dst, sems, index, other)
            sent.append(copy)
            return copy

        slots = len(z_far_first)
        for t in range(slots + 2):
            if t < slots:
                oz = z_far_first[t]
                for h in range(2):
                    near, far = lay.orders[h]
                    by_core[h, oz].wait_recv()
                    for o1 in list(range(1, spans[h][0])) + [0]:
                        for o2 in range(1, spans[h][1]):
                            by_far[h, oz, o1, o2] = forward(
                                h, oz, o1, o2, r_far.at[h, oz, o1, o2 - 1],
                                rs_far, (h, oz, o1, o2), peer(far, o2),
                            )
            if 1 <= t <= slots:
                oz = z_far_first[t - 1]
                for h in range(2):
                    near, far = lay.orders[h]
                    for o1 in range(1, spans[h][0]):
                        for o2 in range(1, spans[h][1]):
                            by_far[h, oz, o1, o2].wait_recv()
                        by_near[h, oz, o1] = forward(
                            h, oz, o1, 0, r_near.at[h, oz, o1 - 1],
                            rs_near, (h, oz, o1), peer(near, o1),
                        )
            if t >= 2:
                oz = z_far_first[t - 2]
                for h in range(2):
                    for o2 in range(1, spans[h][1]):
                        by_far[h, oz, 0, o2].wait_recv()
                    for o1 in range(1, spans[h][0]):
                        by_near[h, oz, o1].wait_recv()
                    if oz:
                        by_z[h, oz] = forward(
                            h, oz, 0, 0, r_z.at[h, oz - 1], rs_z, (h, oz), peer("z", oz)
                        )
        for h in range(2):
            for o in range(1, lay.Z):
                by_z[h, o].wait_recv()
            for i in range(hb):
                m = h * hb + i
                z[:, m * width:(m + 1) * width] = total(h, 0, 0, 0, i)
        for copy in sent:
            copy.wait_send()

    def make_grams(level):
        def one(i, carry):
            pltpu.make_async_copy(left_hbm.at[i], lbuf.at[i], in_sem.at[0, i]).wait()
            pltpu.make_async_copy(right_hbm.at[i], rbuf.at[i], in_sem.at[1, i]).wait()
            gram[i] = lax.dot_general(
                lbuf[i], rbuf[i], (((0,), (0,)), ((), ())), preferred_element_type=jnp.float32
            ).astype(jnp.bfloat16)
            return carry

        lax.fori_loop(level * nb // 4, (level + 1) * nb // 4, one, 0)

    def send_tiles(axis, ref):
        copies = []
        for o in range(1, lay.size[axis]):
            copies.append(
                send(ref, ref, (tile_send, tile_recv), (int(axis == "x"), o), peer(axis, o))
            )
        return copies

    def place_blocks():
        load = pltpu.make_async_copy(tiles, tiles_s, local_sem.at[0])
        load.start()
        load.wait()
        rows, cols = lay.Y * CORES, lay.X * lay.Z
        span = rows * blk
        target = []
        for i in range(nb):
            slot = slot_ref[i]
            owner = slot // cap % cols
            position = tiles_s[owner % lay.X, owner // lay.X, 0, slot % cap]
            row_block, local = position // span, position % span
            target.append(lay.block(row, row_block // blk, row_block % blk))
            target.append(lay.block(local // blk, owner, local % blk))
        number = lax.broadcasted_iota(jnp.int32, last_v.shape, 1)
        last = jnp.full(last_v.shape, 2 * nb, jnp.int32)
        for j, at in enumerate(target):
            pick_ref[j] = at
            before = jnp.int32(2 * nb)
            for i in range(j):
                before = jnp.where(target[i] == at, i, before)
            prev_ref[j] = before
            last = jnp.where(number == at, j, last)
        last_v[...] = last
        store = pltpu.make_async_copy(last_v, last_ref, local_sem.at[1])
        store.start()
        store.wait()

    tiles[me["x"], me["z"]] = tile_ref[...]
    pending = [send_tiles("z", tiles.at[me["x"], me["z"]])]

    def prepare(t):
        if t < 4:
            make_grams(t)
        if t == 1:
            for copy in pending.pop():
                copy.wait()
            pending.append(send_tiles("x", tiles.at[me["x"]]))
        if t == 3:
            for copy in pending.pop():
                copy.wait()
            place_blocks()

    b = b_ref[...]
    put_dots(b * b, d_ref[...] * b * b)
    total = gather(b_ref, prepare)
    first = pick_dot(total, 0)
    beta = jnp.sqrt(first)
    sigma = pick_dot(total, 1) / first
    products()
    scatter_sum()
    v[...] = b_ref[...] / beta
    sv[...] = z[...] / beta
    zero = jnp.zeros_like(beta)
    delta_bar, eps, phi_bar = zero, zero, beta
    cs, sn = -jnp.ones_like(beta), zero
    for step in range(ITERS):
        vv = v[...]
        value = d_ref[...] * vv + sv[...] - sigma * vv
        if step > 0:
            value = value - beta * v_old[...]
        y[...] = value
        put_dots(vv * value, value * value, vv * vv)
        total = gather(y) if step < ITERS - 1 else reduce_dots()
        vy, yy, ones = pick_dot(total, 0), pick_dot(total, 1), pick_dot(total, 2)
        alpha = sigma * ones + vy
        shift = alpha - sigma
        beta_next = jnp.sqrt(jnp.maximum(yy - 2 * shift * vy + shift * shift * ones, 0.0))
        eps_old = eps
        delta = cs * delta_bar + sn * alpha
        gamma_bar = sn * delta_bar - cs * alpha
        eps = sn * beta_next
        delta_bar = -cs * beta_next
        gamma = jnp.sqrt(gamma_bar * gamma_bar + beta_next * beta_next)
        cs = gamma_bar / gamma
        sn = beta_next / gamma
        phi = cs * phi_bar
        phi_bar = sn * phi_bar
        search = v[...]
        if step > 1:
            search = search - eps_old * w_old[...]
        if step > 0:
            search = search - delta * w[...]
            w_old[...] = w[...]
        search = search / gamma
        w[...] = search
        if step == 0:
            out_ref[...] = phi * search
            w_old[...] = jnp.zeros_like(search)
        else:
            out_ref[...] = out_ref[...] + phi * search
        if step < ITERS - 1:
            products()
            scatter_sum()
            v_old[...] = v[...]
            sv[...] = (z[...] - shift * sv[...]) / beta_next
            v[...] = (y[...] - shift * v[...]) / beta_next
            beta, sigma = beta_next, alpha


def body(rows, cols, left, right, bundle_tile_slot, tile_pos, right_sides, diagonal):
    nb, measures, width = left.shape
    nrhs, own = right_sides.shape
    blk = own // width
    lay = Layout(rows, cols, blk)
    cap = tile_pos.shape[-1]
    blocks = blk * rows * cols
    hb = lay.hb
    bf16, f32 = jnp.bfloat16, jnp.float32
    most = max(lay.size.values())

    wide = max(lay.X, lay.Y)
    runs = lay.X * lay.Y * hb

    def landing(*shape):
        return pltpu.VMEM((2, *shape, nrhs, width), bf16)

    counts = ((2, lay.Z), (2, lay.Z, wide), (2, lay.Z, wide, wide), (2, lay.Z))
    sems = [pltpu.SemaphoreType.DMA(shape) for shape in counts for _ in range(2)] * 2
    smem = pl.BlockSpec(memory_space=pltpu.SMEM)
    vmem = pl.BlockSpec(memory_space=pltpu.VMEM)
    hbm = pl.BlockSpec(memory_space=pl.ANY)
    state = pltpu.VMEM((nrhs, own), f32)
    return pl.pallas_call(
        functools.partial(kernel, lay, nb, width, nrhs, blk, cap),
        out_shape=jax.ShapeDtypeStruct((nrhs, own), f32),
        in_specs=[smem, vmem, hbm, hbm, vmem, vmem],
        out_specs=vmem,
        scratch_shapes=[
            pltpu.VMEM((nb, measures, width), bf16),
            pltpu.VMEM((nb, measures, width), bf16),
            pltpu.VMEM((nb, width, width), bf16),
            pltpu.VMEM((blocks, nrhs, width), bf16),
            pltpu.VMEM((blocks, nrhs, width), bf16),
            landing(lay.Z - 1, hb),
            landing(lay.Z, max(wide - 1, 1), hb),
            landing(lay.Z, wide, max(wide - 1, 1), hb),
            landing(lay.Z, runs),
            pltpu.VMEM((2 * nb + 1, nrhs, width), f32),
            pltpu.VMEM((4, most, nrhs, 128), f32),
            state, state, state, state, state, state, state,
            pltpu.VMEM((lay.X, lay.Z, 1, cap), jnp.int32),
            pltpu.SMEM((lay.X, lay.Z, 1, cap), jnp.int32),
            pltpu.VMEM((1, blocks), jnp.int32),
            pltpu.SMEM((1, blocks), jnp.int32),
            pltpu.SMEM((2 * nb,), jnp.int32),
            pltpu.SMEM((2 * nb,), jnp.int32),
            pltpu.SemaphoreType.DMA((2, nb)),
            pltpu.SemaphoreType.DMA((4, most)),
            pltpu.SemaphoreType.DMA((4, most)),
            pltpu.SemaphoreType.DMA((2, most)),
            pltpu.SemaphoreType.DMA((2, most)),
            pltpu.SemaphoreType.DMA((2,)),
            *sems,
        ],
        compiler_params=pltpu.CompilerParams(
            collective_id=0, has_side_effects=True, vmem_limit_bytes=60 * 1024 * 1024
        ),
    )(
        bundle_tile_slot, tile_pos.reshape(1, cap), left, right, right_sides,
        diagonal.reshape(1, own),
    )


def solution(mesh):
    placed = (
        P(("row", "col"), None, None),
        P(("row", "col"), None, None),
        P(("row", "col")),
        P("row", "col", None),
        P(None, ("row", "col")),
        P(("row", "col")),
    )
    return jax.shard_map(
        functools.partial(body, mesh.shape["row"], mesh.shape["col"]),
        mesh=mesh, in_specs=placed, out_specs=P(None, ("row", "col")), check_vma=False,
    )
```

```python
import functools

import jax
import jax.numpy as jnp
from jax import lax
from jax.experimental import pallas as pl
from jax.experimental.pallas import tpu as pltpu
from jax.sharding import PartitionSpec as P

ITERS = 3
CORES = 2
MESH = pl.DeviceIdType.MESH


class Layout:
    def __init__(self, rows, cols, blk):
        self.Y, self.C = rows // CORES, CORES
        x = 1
        while 4 * x * x <= cols:
            x *= 2
        self.X, self.Z = x, cols // x
        self.devices = rows * cols
        self.hb = blk // 2
        self.size = {"z": self.Z, "x": self.X, "y": self.Y, "core": self.C}
        self.orders = (("x", "y"), ("y", "x"))

    def coords(self, row, col):
        return {"z": col // self.X, "x": col % self.X, "y": row // CORES, "core": row % CORES}

    def device(self, c):
        return (c["y"] * CORES + c["core"], c["z"] * self.X + c["x"])

    def chunk(self, half, c):
        near, far = self.orders[half]
        at = c["core"] * self.Z + c["z"]
        return (at * self.size[far] + c[far]) * self.size[near] + c[near]

    def block(self, row, col, m):
        c = self.coords(row, col)
        half = m // self.hb
        at = jnp.where(half == 0, self.chunk(0, c), self.chunk(1, c))
        return (half * self.devices + at) * self.hb + m % self.hb


def kernel(
    lay, nb, width, nrhs, blk, cap,
    slot_ref, tile_ref, left_hbm, right_hbm, b_ref, d_ref, out_ref,
    lbuf, rbuf, gram, xall, part, r_z, r_near, r_far, r_core, acc, dots,
    v, v_old, sv, y, w, w_old, z,
    tiles, tiles_s, last_v, last_ref, pick_ref, prev_ref,
    in_sem, dot_send, dot_recv, tile_send, tile_recv, local_sem, *sems,
):
    row, col = lax.axis_index("row"), lax.axis_index("col")
    me = lay.coords(row, col)
    hb = lay.hb
    half_blocks = lay.devices * hb
    ag_z, ag_near, ag_far, ag_core = [sems[i:i + 2] for i in range(0, 8, 2)]
    rs_z, rs_near, rs_far, rs_core = [sems[i:i + 2] for i in range(8, 16, 2)]

    def peer(axis, offset):
        other = dict(me)
        other[axis] = lax.rem(me[axis] + offset, lay.size[axis])
        return other

    for i in range(nb):
        pltpu.make_async_copy(left_hbm.at[i], lbuf.at[i], in_sem.at[0, i]).start()
        pltpu.make_async_copy(right_hbm.at[i], rbuf.at[i], in_sem.at[1, i]).start()

    barrier = pltpu.get_barrier_semaphore()
    greeted = 0
    for axis in ("z", "x", "y", "core"):
        for o in range(1, lay.size[axis]):
            pl.semaphore_signal(
                barrier, inc=1, device_id=lay.device(peer(axis, o)), device_id_type=MESH
            )
            greeted += 1
    pl.semaphore_wait(barrier, greeted)

    dot_axes = ("z", "x", "y", "core")
    lane = lax.broadcasted_iota(jnp.int32, (nrhs, 128), 1)

    def put_dots(*values):
        tile = jnp.zeros((nrhs, 128), jnp.float32)
        for j, value in enumerate(values):
            tile = jnp.where(lane == j, jnp.sum(value, axis=1, keepdims=True), tile)
        dots[0, me["z"]] = tile

    def start_dots(level):
        copies = []
        axis = dot_axes[level]
        for o in range(1, lay.size[axis]):
            src = dots.at[level, me[axis]]
            copy = pltpu.make_async_remote_copy(
                src_ref=src, dst_ref=src,
                send_sem=dot_send.at[level, o], recv_sem=dot_recv.at[level, o],
                device_id=lay.device(peer(axis, o)), device_id_type=MESH,
            )
            copy.start()
            copies.append(copy)
        return copies

    def sum_dots(level):
        total = dots[level, 0]
        for s in range(1, lay.size[dot_axes[level]]):
            total = total + dots[level, s]
        if level < 3:
            dots[level + 1, me[dot_axes[level + 1]]] = total
        return total

    def pick_dot(total, j):
        return jnp.sum(jnp.where(lane == j, total, 0.0), axis=1, keepdims=True)

    def place(h, oz=0, o1=0, o2=0, other_core=False):
        near, far = lay.orders[h]
        c = dict(me)
        for axis, o in (("z", oz), (near, o1), (far, o2)):
            if o:
                c[axis] = lax.rem(me[axis] + o, lay.size[axis])
        if other_core:
            c["core"] = 1 - me["core"]
        return h * half_blocks + lay.chunk(h, c) * hb

    def group(h, oz, other_core=False):
        c = dict(me, z=lax.rem(me["z"] + oz, lay.Z), x=0, y=0)
        if other_core:
            c["core"] = 1 - me["core"]
        return h * half_blocks + lay.chunk(h, c) * hb

    def send(src, dst, sems, index, other):
        copy = pltpu.make_async_remote_copy(
            src_ref=src, dst_ref=dst, send_sem=sems[0].at[index], recv_sem=sems[1].at[index],
            device_id=lay.device(other), device_id_type=MESH,
        )
        copy.start()
        return copy

    spans = [[lay.size[axis] for axis in order] for order in lay.orders]
    run = lay.X * lay.Y * hb
    z_near_first = sorted(range(1, lay.Z), key=lambda o: (min(o, lay.Z - o), o))

    def gather(x_ref, hook=None):
        for m in range(blk):
            h = m // hb
            xall[place(h) + m % hb] = x_ref[:, m * width:(m + 1) * width].astype(jnp.bfloat16)
        sent = []

        def push(at, count, sems, index, other):
            ref = xall.at[pl.ds(at, count)]
            copy = send(ref, ref, sems, index, other)
            sent.append(copy)
            return copy

        small = start_dots(0)
        by_z, by_near, by_far, by_core = {}, {}, {}, []
        for o in z_near_first:
            for h in range(2):
                by_z[h, o] = push(place(h), hb, ag_z, (h, o), peer("z", o))
        order = [0] + z_near_first
        slots = len(order)
        for t in range(slots + 2):
            if t < slots:
                o = order[t]
                oz = (lay.Z - o) % lay.Z
                for h in range(2):
                    if o:
                        by_z[h, o].wait_recv()
                    near, far = lay.orders[h]
                    for o1 in range(1, spans[h][0]):
                        by_near[h, oz, o1] = push(
                            place(h, oz), hb, ag_near, (h, oz, o1), peer(near, o1)
                        )
                    for o2 in range(1, spans[h][1]):
                        by_far[h, oz, 0, o2] = push(
                            place(h, oz), hb, ag_far, (h, oz, 0, o2), peer(far, o2)
                        )
            if 1 <= t <= slots:
                oz = (lay.Z - order[t - 1]) % lay.Z
                for h in range(2):
                    near, far = lay.orders[h]
                    for o1 in range(1, spans[h][0]):
                        by_near[h, oz, o1].wait_recv()
                        back = spans[h][0] - o1
                        for o2 in range(1, spans[h][1]):
                            by_far[h, oz, back, o2] = push(
                                place(h, oz, back), hb, ag_far, (h, oz, back, o2), peer(far, o2)
                            )
            if t >= 2:
                oz = (lay.Z - order[t - 2]) % lay.Z
                for h in range(2):
                    for o1 in range(spans[h][0]):
                        for o2 in range(1, spans[h][1]):
                            by_far[h, oz, o1, o2].wait_recv()
                    by_core.append(push(group(h, oz), run, ag_core, (h, oz), peer("core", 1)))
            if hook is not None:
                hook(t)
            level = {slots - 1: 0, slots: 1, slots + 1: 2}.get(t)
            if level is not None:
                for copy in small:
                    copy.wait()
                sum_dots(level)
                small = start_dots(level + 1)
        for copy in by_core:
            copy.wait_recv()
        for copy in sent:
            copy.wait_send()
        for copy in small:
            copy.wait()
        return sum_dots(3)

    def reduce_dots():
        total = None
        for level in range(4):
            for copy in start_dots(level):
                copy.wait()
            total = sum_dots(level)
        return total

    def products():
        acc[2 * nb] = jnp.zeros((nrhs, width), jnp.float32)

        for i in range(nb):
            g = gram[i]
            x_row = xall[pick_ref[2 * i]]
            x_col = xall[pick_ref[2 * i + 1]]
            acc[2 * i] = lax.dot_general(
                x_col, g, (((1,), (1,)), ((), ())), preferred_element_type=jnp.float32
            )
            acc[2 * i + 1] = jnp.dot(x_row, g, preferred_element_type=jnp.float32)
        for j in range(1, 2 * nb):
            acc[j] = acc[j] + acc[prev_ref[j]]

    def scatter_sum():
        sent = []
        z_far_first = z_near_first[::-1] + [0]
        by_core, by_far, by_near, by_z = {}, {}, {}, {}
        for oz in z_far_first:
            for h in range(2):
                at = group(h, oz, True)

                def spread(i, carry):
                    for u in range(2):
                        k = at + 2 * i + u
                        part[k] = acc[last_ref[0, k]].astype(jnp.bfloat16)
                    return carry

                lax.fori_loop(0, run // 2, spread, 0)
                by_core[h, oz] = send(
                    part.at[pl.ds(at, run)], r_core.at[h, oz], rs_core, (h, oz), peer("core", 1)
                )
                sent.append(by_core[h, oz])

        def total(h, oz, o1, o2, i):
            at = place(h, oz, o1, o2) + i
            value = acc[last_ref[0, at]] + r_core[h, oz, at - group(h, oz)].astype(jnp.float32)
            if o2 == 0:
                for o in range(1, spans[h][1]):
                    value = value + r_far[h, oz, o1, o - 1, i].astype(jnp.float32)
                if o1 == 0:
                    for o in range(1, spans[h][0]):
                        value = value + r_near[h, oz, o - 1, i].astype(jnp.float32)
                    if oz == 0:
                        for o in range(1, lay.Z):
                            value = value + r_z[h, o - 1, i].astype(jnp.float32)
            return value

        def forward(h, oz, o1, o2, dst, sems, index, other):
            at = place(h, oz, o1, o2)
            for i in range(hb):
                part[at + i] = total(h, oz, o1, o2, i).astype(jnp.bfloat16)
            copy = send(part.at[pl.ds(at, hb)], dst, sems, index, other)
            sent.append(copy)
            return copy

        slots = len(z_far_first)
        for t in range(slots + 2):
            if t < slots:
                oz = z_far_first[t]
                for h in range(2):
                    near, far = lay.orders[h]
                    by_core[h, oz].wait_recv()
                    for o1 in list(range(1, spans[h][0])) + [0]:
                        for o2 in range(1, spans[h][1]):
                            by_far[h, oz, o1, o2] = forward(
                                h, oz, o1, o2, r_far.at[h, oz, o1, o2 - 1],
                                rs_far, (h, oz, o1, o2), peer(far, o2),
                            )
            if 1 <= t <= slots:
                oz = z_far_first[t - 1]
                for h in range(2):
                    near, far = lay.orders[h]
                    for o1 in range(1, spans[h][0]):
                        for o2 in range(1, spans[h][1]):
                            by_far[h, oz, o1, o2].wait_recv()
                        by_near[h, oz, o1] = forward(
                            h, oz, o1, 0, r_near.at[h, oz, o1 - 1],
                            rs_near, (h, oz, o1), peer(near, o1),
                        )
            if t >= 2:
                oz = z_far_first[t - 2]
                for h in range(2):
                    for o2 in range(1, spans[h][1]):
                        by_far[h, oz, 0, o2].wait_recv()
                    for o1 in range(1, spans[h][0]):
                        by_near[h, oz, o1].wait_recv()
                    if oz:
                        by_z[h, oz] = forward(
                            h, oz, 0, 0, r_z.at[h, oz - 1], rs_z, (h, oz), peer("z", oz)
                        )
        for h in range(2):
            for o in range(1, lay.Z):
                by_z[h, o].wait_recv()
            for i in range(hb):
                m = h * hb + i
                z[:, m * width:(m + 1) * width] = total(h, 0, 0, 0, i)
        for copy in sent:
            copy.wait_send()

    def make_grams(level):
        def one(i, carry):
            pltpu.make_async_copy(left_hbm.at[i], lbuf.at[i], in_sem.at[0, i]).wait()
            pltpu.make_async_copy(right_hbm.at[i], rbuf.at[i], in_sem.at[1, i]).wait()
            gram[i] = lax.dot_general(
                lbuf[i], rbuf[i], (((0,), (0,)), ((), ())), preferred_element_type=jnp.float32
            ).astype(jnp.bfloat16)
            return carry

        lax.fori_loop(level * nb // 4, (level + 1) * nb // 4, one, 0)

    def send_tiles(axis, ref):
        copies = []
        for o in range(1, lay.size[axis]):
            copies.append(
                send(ref, ref, (tile_send, tile_recv), (int(axis == "x"), o), peer(axis, o))
            )
        return copies

    def place_blocks():
        load = pltpu.make_async_copy(tiles, tiles_s, local_sem.at[0])
        load.start()
        load.wait()
        rows, cols = lay.Y * CORES, lay.X * lay.Z
        span = rows * blk
        target = []
        for i in range(nb):
            slot = slot_ref[i]
            owner = slot // cap % cols
            position = tiles_s[owner % lay.X, owner // lay.X, 0, slot % cap]
            row_block, local = position // span, position % span
            target.append(lay.block(row, row_block // blk, row_block % blk))
            target.append(lay.block(local // blk, owner, local % blk))
        number = lax.broadcasted_iota(jnp.int32, last_v.shape, 1)
        last = jnp.full(last_v.shape, 2 * nb, jnp.int32)
        for j, at in enumerate(target):
            pick_ref[j] = at
            before = jnp.int32(2 * nb)
            for i in range(j):
                before = jnp.where(target[i] == at, i, before)
            prev_ref[j] = before
            last = jnp.where(number == at, j, last)
        last_v[...] = last
        store = pltpu.make_async_copy(last_v, last_ref, local_sem.at[1])
        store.start()
        store.wait()

    tiles[me["x"], me["z"]] = tile_ref[...]
    pending = [send_tiles("z", tiles.at[me["x"], me["z"]])]

    def prepare(t):
        if t < 4:
            make_grams(t)
        if t == 1:
            for copy in pending.pop():
                copy.wait()
            pending.append(send_tiles("x", tiles.at[me["x"]]))
        if t == lay.Z + 1:
            for copy in pending.pop():
                copy.wait()
            place_blocks()

    b = b_ref[...]
    put_dots(b * b, d_ref[...] * b * b)
    total = gather(b_ref, prepare)
    first = pick_dot(total, 0)
    beta = jnp.sqrt(first)
    sigma = pick_dot(total, 1) / first
    products()
    scatter_sum()
    v[...] = b_ref[...] / beta
    sv[...] = z[...] / beta
    zero = jnp.zeros_like(beta)
    delta_bar, eps, phi_bar = zero, zero, beta
    cs, sn = -jnp.ones_like(beta), zero
    for step in range(ITERS):
        vv = v[...]
        value = d_ref[...] * vv + sv[...] - sigma * vv
        if step > 0:
            value = value - beta * v_old[...]
        y[...] = value
        put_dots(vv * value, value * value, vv * vv)
        total = gather(y) if step < ITERS - 1 else reduce_dots()
        vy, yy, ones = pick_dot(total, 0), pick_dot(total, 1), pick_dot(total, 2)
        alpha = sigma * ones + vy
        shift = alpha - sigma
        beta_next = jnp.sqrt(jnp.maximum(yy - 2 * shift * vy + shift * shift * ones, 0.0))
        eps_old = eps
        delta = cs * delta_bar + sn * alpha
        gamma_bar = sn * delta_bar - cs * alpha
        eps = sn * beta_next
        delta_bar = -cs * beta_next
        gamma = jnp.sqrt(gamma_bar * gamma_bar + beta_next * beta_next)
        cs = gamma_bar / gamma
        sn = beta_next / gamma
        phi = cs * phi_bar
        phi_bar = sn * phi_bar
        search = v[...]
        if step > 1:
            search = search - eps_old * w_old[...]
        if step > 0:
            search = search - delta * w[...]
            w_old[...] = w[...]
        search = search / gamma
        w[...] = search
        if step == 0:
            out_ref[...] = phi * search
            w_old[...] = jnp.zeros_like(search)
        else:
            out_ref[...] = out_ref[...] + phi * search
        if step < ITERS - 1:
            products()
            scatter_sum()
            v_old[...] = v[...]
            sv[...] = (z[...] - shift * sv[...]) / beta_next
            v[...] = (y[...] - shift * v[...]) / beta_next
            beta, sigma = beta_next, alpha


def body(rows, cols, left, right, bundle_tile_slot, tile_pos, right_sides, diagonal):
    nb, measures, width = left.shape
    nrhs, own = right_sides.shape
    blk = own // width
    lay = Layout(rows, cols, blk)
    cap = tile_pos.shape[-1]
    blocks = blk * rows * cols
    hb = lay.hb
    bf16, f32 = jnp.bfloat16, jnp.float32
    most = max(lay.size.values())

    wide = max(lay.X, lay.Y)
    runs = lay.X * lay.Y * hb

    def landing(*shape):
        return pltpu.VMEM((2, *shape, nrhs, width), bf16)

    counts = ((2, lay.Z), (2, lay.Z, wide), (2, lay.Z, wide, wide), (2, lay.Z))
    sems = [pltpu.SemaphoreType.DMA(shape) for shape in counts for _ in range(2)] * 2
    smem = pl.BlockSpec(memory_space=pltpu.SMEM)
    vmem = pl.BlockSpec(memory_space=pltpu.VMEM)
    hbm = pl.BlockSpec(memory_space=pl.ANY)
    state = pltpu.VMEM((nrhs, own), f32)
    return pl.pallas_call(
        functools.partial(kernel, lay, nb, width, nrhs, blk, cap),
        out_shape=jax.ShapeDtypeStruct((nrhs, own), f32),
        in_specs=[smem, vmem, hbm, hbm, vmem, vmem],
        out_specs=vmem,
        scratch_shapes=[
            pltpu.VMEM((nb, measures, width), bf16),
            pltpu.VMEM((nb, measures, width), bf16),
            pltpu.VMEM((nb, width, width), bf16),
            pltpu.VMEM((blocks, nrhs, width), bf16),
            pltpu.VMEM((blocks, nrhs, width), bf16),
            landing(lay.Z - 1, hb),
            landing(lay.Z, max(wide - 1, 1), hb),
            landing(lay.Z, wide, max(wide - 1, 1), hb),
            landing(lay.Z, runs),
            pltpu.VMEM((2 * nb + 1, nrhs, width), f32),
            pltpu.VMEM((4, most, nrhs, 128), f32),
            state, state, state, state, state, state, state,
            pltpu.VMEM((lay.X, lay.Z, 1, cap), jnp.int32),
            pltpu.SMEM((lay.X, lay.Z, 1, cap), jnp.int32),
            pltpu.VMEM((1, blocks), jnp.int32),
            pltpu.SMEM((1, blocks), jnp.int32),
            pltpu.SMEM((2 * nb,), jnp.int32),
            pltpu.SMEM((2 * nb,), jnp.int32),
            pltpu.SemaphoreType.DMA((2, nb)),
            pltpu.SemaphoreType.DMA((4, most)),
            pltpu.SemaphoreType.DMA((4, most)),
            pltpu.SemaphoreType.DMA((2, most)),
            pltpu.SemaphoreType.DMA((2, most)),
            pltpu.SemaphoreType.DMA((2,)),
            *sems,
        ],
        compiler_params=pltpu.CompilerParams(
            collective_id=0, has_side_effects=True, vmem_limit_bytes=60 * 1024 * 1024
        ),
    )(
        bundle_tile_slot, tile_pos.reshape(1, cap), left, right, right_sides,
        diagonal.reshape(1, own),
    )


def solution(mesh):
    placed = (
        P(("row", "col"), None, None),
        P(("row", "col"), None, None),
        P(("row", "col")),
        P("row", "col", None),
        P(None, ("row", "col")),
        P(("row", "col")),
    )
    return jax.shard_map(
        functools.partial(body, mesh.shape["row"], mesh.shape["col"]),
        mesh=mesh, in_specs=placed, out_specs=P(None, ("row", "col")), check_vma=False,
    )
```
